32 devices in a mesh: obs: 4 (over y, core), flux: 8 (over z, x).
Axes of the slice: x: 2, y: 2, z: 4, core: 2. Of those that a mesh axis runs over, the one named last changes fastest.
Arguments:
- jacobian: bfloat16 [512, 8192], P('obs', 'flux'), may hold values from -0.0625 to 0.0625
- probes: bfloat16 [2, 8192, 128], P(None, 'flux'), may hold values from -6 to 6
- prior_std: float32 [8192], P('flux'), may hold values from 0.5 to 2
- obs_weight: float32 [512], P('obs'), may hold values from 0.25 to 4
Outputs:
- sketch: float32 [8192, 256], P(('flux', 'obs'))
- basis_out: float32 [8192, 256], P(('flux', 'obs'))
The draws below stay inside these ranges and needn't reach their ends.
All inputs are finite; a program needn't handle non-finite values.
Results may differ from the reference program's by a relative error of at most 0.005.
Values may be sent and summed in bfloat16 or wider, within the bound.
A program may use at most 64 MiB of HBM per device.

```python
import math
import jax
import jax.numpy as jnp
from jax import lax

P_SIZE = 128
NB = 2
OBS = 512
FLUX = 8192


def level_of(own_key, extent, shards, least, high):
    loudness, own = 1.0, jax.random.fold_in(own_key, 6)
    for axis_at, parts in shards:
        steps = jnp.exp(jax.random.uniform(jax.random.fold_in(own, axis_at), (parts,), jnp.float32, least / len(shards), high / len(shards)))
        loudness = loudness * jnp.repeat(steps, extent[axis_at] // parts).reshape([-1 if axis == axis_at else 1 for axis in range(len(extent))])
    return loudness


def noise(own_key, dims, scale, limit, pieces=(), dtype=jnp.bfloat16):
    entries = scale * jax.random.normal(own_key, dims, jnp.float32)
    if pieces:
        entries = entries * level_of(own_key, dims, pieces, -0.22, 0.18)
    return jnp.clip(entries, -limit, limit).astype(dtype)


def setup_inputs(seed: int = 0) -> dict:
    splits = jax.random.split(jax.random.key(seed), 5)
    return {
        "jacobian": noise(splits[0], (OBS, FLUX), FLUX ** -0.5, 0.0625, ((0, 4), (1, 8))),
        "probes": noise(splits[1], (NB, FLUX, P_SIZE), 1.0, 6.0, ((1, 8),)),
        "prior_std": jnp.clip(jnp.exp(math.log(2.0) - 1.3862944 * jax.random.uniform(splits[2], (FLUX,), jnp.float32) ** level_of(splits[2], (FLUX,), ((0, 8),), -0.2, 0.2)), 0.5, 2.0),
        "obs_weight": jnp.clip(jnp.exp(math.log(4.0) - 2.7725887 * jax.random.uniform(splits[3], (OBS,), jnp.float32) ** level_of(splits[3], (OBS,), ((0, 4),), -0.2, 0.2)), 0.25, 4.0),
    }


def reference(jacobian, probes, prior_std, obs_weight):
    column_total = NB * P_SIZE
    stacked = jnp.transpose(probes.astype(jnp.float32), (1, 0, 2)).reshape(FLUX, column_total)
    stacked = (stacked * prior_std[:, None]).astype(jnp.bfloat16)
    forward = jnp.dot(jacobian.astype(jnp.float32), stacked.astype(jnp.float32), preferred_element_type=jnp.float32)
    weighted = (forward * obs_weight[:, None]).astype(jnp.bfloat16)
    adjoint = lax.dot_general(jacobian.astype(jnp.float32), weighted.astype(jnp.float32), (((0,), (0,)), ((), ())), preferred_element_type=jnp.float32)
    sketch = adjoint * prior_std[:, None]
    gram_matrix = jnp.dot(sketch.T.astype(jnp.float32), sketch.astype(jnp.float32), precision=lax.Precision.HIGHEST, preferred_element_type=jnp.float32)
    factor = jnp.linalg.cholesky(gram_matrix)
    basis_out = jax.scipy.linalg.solve_triangular(factor, sketch.T, lower=True).T * math.sqrt(FLUX)
    return (sketch, basis_out)
```

```python
import functools
import math

import jax
import jax.numpy as jnp
from jax import lax
from jax.experimental import pallas as pl
from jax.experimental.pallas import tpu as pltpu
from jax.sharding import PartitionSpec as P

MESH = pl.DeviceIdType.MESH
HIGHEST = lax.Precision.HIGHEST
F32 = jnp.float32
BF16 = jnp.bfloat16
LANES = 128
PANEL = 32


def each(lower, upper, step):
    if upper - lower <= 16:
        for value in range(lower, upper):
            step(value)
    else:
        lax.fori_loop(lower, upper, lambda value, carry: (step(value), carry)[1], 0)


def only(condition, step):
    if condition is True:
        step()
    else:
        pl.when(condition)(step)


def wait_bytes(ref, sem):
    pltpu.make_async_copy(ref, ref, sem).wait()


def column(row):
    return jnp.broadcast_to(row, (LANES, LANES)).T


def factor_inverse(work, width):
    for start in range(0, width, PANEL):
        stop = start + PANEL
        left = start // LANES * LANES
        right = width + (stop + LANES - 1) // LANES * LANES
        rows = work[start:stop, left:right]
        index = lax.broadcasted_iota(jnp.int32, (PANEL, 1), 0)
        diagonal = jnp.zeros((PANEL, 1), F32)
        for k in range(PANEL):
            at = start - left + k
            pivot_row = rows[k : k + 1, :]
            multiplier = rows[:, at : at + 1]
            pivot = multiplier[k : k + 1, :]
            diagonal = jnp.where(index == k, pivot, diagonal)
            scaled = jnp.where(index > k, multiplier, 0.0) * (1.0 / pivot)
            rows = rows - scaled * pivot_row
        rows = rows * (1.0 / jnp.sqrt(diagonal))
        work[start:stop, left:right] = rows
        if stop < width:
            update = lax.dot_general(
                rows[:, : width - left],
                rows,
                (((0,), (0,)), ((), ())),
                precision=HIGHEST,
                preferred_element_type=F32,
            )
            work[stop:width, left:right] = work[stop:width, left:right] - update[stop - left :, :]


def kernel(
    sizes, jac, probes, std, weight, sketch_out, basis_out,
    std_col, weight_col, stacked, jt, jrecv, fsend, frecv, wbuf,
    gsend, gpair, gchunk, grecv, gfull, work, send_sems, recv_sems,
):
    n_obs, n_flux, scale = sizes
    blocks, flux_local, probe_count = probes.shape
    obs_local = jac.shape[0]
    width = blocks * probe_count
    portion = flux_local // n_obs
    n_y = n_obs // 2
    chips = n_y * n_flux
    w_owners, w_rows = fsend.shape[0], fsend.shape[1]
    g_owners = gsend.shape[1]

    o, f = lax.axis_index("obs"), lax.axis_index("flux")
    core, y = lax.rem(o, 2), o // 2
    chip = y * n_flux + f
    partner = (o + 1 - 2 * core, f)
    w_mine = True if w_owners == n_flux else f < w_owners
    g_mine = True if g_owners == chips else chip < g_owners

    def on_chip(step, c):
        other = lax.rem(chip + step, chips)
        return other, ((other // n_flux) * 2 + c, lax.rem(other, n_flux))

    barrier = pltpu.get_barrier_semaphore()

    def greet(step):
        _, device = on_chip(step, core)
        pl.semaphore_signal(barrier, inc=1, device_id=device, device_id_type=MESH)

    def greet_other(step):
        _, device = on_chip(step, 1 - core)
        pl.semaphore_signal(barrier, inc=1, device_id=device, device_id_type=MESH)

    each(1, chips, greet)
    each(0, chips, greet_other)

    for s in range(flux_local // LANES):
        part = slice(s * LANES, (s + 1) * LANES)
        std_col[part, :] = column(std[:, part])
    for s in range(obs_local // LANES):
        part = slice(s * LANES, (s + 1) * LANES)
        weight_col[part, :] = column(weight[:, part])
    for b in range(blocks):
        stacked[:, b * probe_count : (b + 1) * probe_count] = (
            probes[b].astype(F32) * std_col[...]
        ).astype(BF16)
    partial = jnp.dot(jac[...], stacked[...], preferred_element_type=F32)
    fsend[...] = partial.reshape(w_owners, w_rows, width)
    jt[...] = jac[...].T.reshape(n_obs, portion, obs_local)

    pl.semaphore_wait(barrier, 2 * chips - 1)

    def send(src, dst, number, device):
        copy = pltpu.make_async_remote_copy(
            src_ref=src, dst_ref=dst, send_sem=send_sems.at[number],
            recv_sem=recv_sems.at[number], device_id=device, device_id_type=MESH,
        )
        copy.start()
        return copy

    def send_forward(step):
        other = lax.rem(f + step, n_flux)
        only(
            True if w_owners == n_flux else other < w_owners,
            lambda: send(fsend.at[other], frecv.at[f], 0, (o, other)) and None,
        )

    each(1, n_flux, send_forward)

    def send_jacobian(step):
        other = lax.rem(o + step, n_obs)
        send(jt.at[other], jrecv.at[core, y], 1, (other, f))

    each(1, n_obs, send_jacobian)
    jrecv[core, y] = jt[o]

    def weigh():
        frecv[f] = fsend[f]
        wait_bytes(frecv.at[pl.ds(0, n_flux - 1)], recv_sems.at[0])
        rows = jnp.sum(frecv[...], axis=0)
        at = pl.ds(pl.multiple_of(f * w_rows, w_rows), w_rows)
        factor = jnp.concatenate([weight_col[at, :]] * (width // LANES), axis=1)
        mine = y * w_owners + f
        wbuf[core, mine] = (rows * factor).astype(BF16)

        def share(step):
            _, device = on_chip(step, core)
            send(wbuf.at[core, mine], wbuf.at[core, mine], 2, device)

        each(1, chips, share)

    only(w_mine, weigh)
    w_total = n_y * w_owners
    if w_mine is True:
        wait_bytes(wbuf.at[core, pl.ds(0, w_total - 1)], recv_sems.at[2])
    else:
        pl.when(w_mine)(lambda: wait_bytes(wbuf.at[core, pl.ds(0, w_total - 1)], recv_sems.at[2]))
        pl.when(f >= w_owners)(lambda: wait_bytes(wbuf.at[core], recv_sems.at[2]))
    across = send(wbuf.at[core], wbuf.at[core], 3, partner)

    wait_bytes(jt.at[pl.ds(0, n_obs - 1)], recv_sems.at[1])

    def adjoint(c):
        total = jnp.zeros((portion, width), F32)
        for row in range(n_y):
            piece = wbuf[c, row * w_owners : (row + 1) * w_owners].reshape(obs_local, width)
            total = total + jnp.dot(jrecv[c, row], piece, preferred_element_type=F32)
        return total

    own_half = adjoint(core)
    across.wait_recv()
    total = own_half + adjoint(1 - core)
    at = pl.ds(pl.multiple_of(o * portion, portion), portion)
    sketch = total * jnp.concatenate([std_col[at, :]] * (width // LANES), axis=1)
    sketch_out[...] = sketch
    gram = lax.dot_general(
        sketch, sketch, (((0,), (0,)), ((), ())), precision=HIGHEST, preferred_element_type=F32
    )
    gsend[...] = gram.reshape(gsend.shape)

    pair = send(gsend.at[1 - core], gpair, 4, partner)
    pair.wait_recv()
    gchunk[...] = gsend[core] + gpair[...]

    def send_gram(step):
        other, device = on_chip(step, core)
        only(
            True if g_owners == chips else other < g_owners,
            lambda: send(gchunk.at[other], grecv.at[chip], 5, device) and None,
        )

    each(1, chips, send_gram)

    def total_gram():
        grecv[chip] = gchunk[chip]
        wait_bytes(grecv.at[pl.ds(0, chips - 1)], recv_sems.at[5])
        gfull[core, chip] = jnp.sum(grecv[...], axis=0)

        def share(step):
            _, device = on_chip(step, core)
            send(gfull.at[core, chip], gfull.at[core, chip], 6, device)

        each(1, chips, share)

    only(g_mine, total_gram)
    if g_mine is True:
        wait_bytes(gfull.at[core, pl.ds(0, g_owners - 1)], recv_sems.at[6])
    else:
        pl.when(g_mine)(lambda: wait_bytes(gfull.at[core, pl.ds(0, g_owners - 1)], recv_sems.at[6]))
        pl.when(chip >= g_owners)(lambda: wait_bytes(gfull.at[core], recv_sems.at[6]))
    gacross = send(gfull.at[core], gfull.at[core], 7, partner)
    gacross.wait_recv()

    work[:, :width] = gfull[...].reshape(width, width)
    work[:, width:] = (
        lax.broadcasted_iota(jnp.int32, (width, width), 0)
        == lax.broadcasted_iota(jnp.int32, (width, width), 1)
    ).astype(F32)
    factor_inverse(work, width)
    basis = lax.dot_general(
        sketch_out[...], work[:, width:], (((1,), (1,)), ((), ())),
        precision=HIGHEST, preferred_element_type=F32,
    )
    basis_out[...] = basis * scale

    if w_mine is True:
        wait_bytes(fsend.at[pl.ds(0, w_owners - 1)], send_sems.at[0])
        wait_bytes(grecv.at[pl.ds(0, 0 + chips - 1)], send_sems.at[5])
    else:
        pl.when(w_mine)(lambda: wait_bytes(fsend.at[pl.ds(0, w_owners - 1)], send_sems.at[0]))
        pl.when(f >= w_owners)(lambda: wait_bytes(fsend, send_sems.at[0]))
        pl.when(g_mine)(lambda: wait_bytes(gchunk.at[pl.ds(0, g_owners - 1)], send_sems.at[5]))
        pl.when(chip >= g_owners)(lambda: wait_bytes(gchunk, send_sems.at[5]))
    wait_bytes(jt.at[pl.ds(0, n_obs - 1)], send_sems.at[1])

    def w_sent():
        each(1, chips, lambda step: wait_bytes(wbuf.at[core, 0], send_sems.at[2]))

    only(w_mine, w_sent)
    across.wait_send()
    pair.wait_send()

    def g_sent():
        each(1, chips, lambda step: wait_bytes(gfull.at[core, 0], send_sems.at[6]))

    only(g_mine, g_sent)
    gacross.wait_send()


def body(jacobian, probes, prior_std, obs_weight):
    blocks, flux_local, probe_count = probes.shape
    obs_local = jacobian.shape[0]
    n_obs, n_flux = lax.axis_size("obs"), lax.axis_size("flux")
    width = blocks * probe_count
    portion = flux_local // n_obs
    chips = n_obs // 2 * n_flux
    w_rows = max(16, obs_local // n_flux)
    w_owners = obs_local // w_rows
    g_rows = max(8, width // 2 // chips)
    g_owners = width // 2 // g_rows
    scale = math.sqrt(flux_local * n_flux)
    vmem = pl.BlockSpec(memory_space=pltpu.VMEM)
    out = jax.ShapeDtypeStruct((portion, width), F32)
    return pl.pallas_call(
        functools.partial(kernel, (n_obs, n_flux, scale)),
        out_shape=(out, out),
        in_specs=[vmem] * 4,
        out_specs=(vmem, vmem),
        scratch_shapes=[
            pltpu.VMEM((flux_local, LANES), F32),
            pltpu.VMEM((obs_local, LANES), F32),
            pltpu.VMEM((flux_local, width), BF16),
            pltpu.VMEM((n_obs, portion, obs_local), BF16),
            pltpu.VMEM((2, n_obs // 2, portion, obs_local), BF16),
            pltpu.VMEM((w_owners, w_rows, width), F32),
            pltpu.VMEM((n_flux, w_rows, width), F32),
            pltpu.VMEM((2, n_obs // 2 * w_owners, w_rows, width), BF16),
            pltpu.VMEM((2, g_owners, g_rows, width), F32),
            pltpu.VMEM((g_owners, g_rows, width), F32),
            pltpu.VMEM((g_owners, g_rows, width), F32),
            pltpu.VMEM((chips, g_rows, width), F32),
            pltpu.VMEM((2, g_owners, g_rows, width), F32),
            pltpu.VMEM((width, 2 * width), F32),
            pltpu.SemaphoreType.DMA((8,)),
            pltpu.SemaphoreType.DMA((8,)),
        ],
        compiler_params=pltpu.CompilerParams(collective_id=0, has_side_effects=True),
    )(jacobian, probes, prior_std.reshape(1, -1), obs_weight.reshape(1, -1))


def solution(mesh):
    in_specs = (P("obs", "flux"), P(None, "flux", None), P("flux"), P("obs"))
    out_specs = (P(("flux", "obs"), None), P(("flux", "obs"), None))
    return jax.shard_map(body, mesh=mesh, in_specs=in_specs, out_specs=out_specs, check_vma=False)
```

```python
import functools
import math

import jax
import jax.numpy as jnp
from jax import lax
from jax.experimental import pallas as pl
from jax.experimental.pallas import tpu as pltpu
from jax.sharding import PartitionSpec as P

MESH = pl.DeviceIdType.MESH
HIGHEST = lax.Precision.HIGHEST
F32 = jnp.float32
BF16 = jnp.bfloat16
LANES = 128
PANEL = 64
TILE = 8


def each(lower, upper, step):
    if upper - lower <= 16:
        for value in range(lower, upper):
            step(value)
    else:
        lax.fori_loop(lower, upper, lambda value, carry: (step(value), carry)[1], 0)


def only(condition, step):
    if condition is True:
        step()
    else:
        pl.when(condition)(step)


def wait_bytes(ref, sem):
    pltpu.make_async_copy(ref, ref, sem).wait()


def column(row):
    return jnp.broadcast_to(row, (LANES, LANES)).T


def factor_rows(work, start, stop, width):
    index = lax.broadcasted_iota(jnp.int32, (TILE, LANES), 0)

    def spread(x, k):
        return jnp.broadcast_to(x[k : k + 1, :], x.shape)

    def columns(x, at):
        return [jnp.broadcast_to(x[:, at + j : at + j + 1], (TILE, LANES)) for j in range(TILE)]

    for first in range(start, stop, TILE):
        left = first // LANES * LANES
        right = width + left + LANES
        spans = [slice(s, s + LANES) for s in range(0, right - left, LANES)]
        top = work[first : first + TILE, left:right]
        cols = columns(top, first - left)
        parts = [top[:, span] for span in spans]
        steps = []
        diagonal = jnp.ones((TILE, LANES), F32)
        for k in range(TILE):
            pivot = spread(cols[k], k)
            diagonal = jnp.where(index == k, pivot, diagonal)
            inverse = 1.0 / pivot
            pivot_row = [spread(part, k) for part in parts]
            heads = [spread(col, k) for col in cols]
            steps.append((inverse, pivot_row, heads))
            if k < TILE - 1:
                multiplier = jnp.where(index > k, cols[k], 0.0) * inverse
                for j in range(k + 1, TILE):
                    cols[j] = cols[j] - multiplier * heads[j]
                parts = [part - multiplier * row for part, row in zip(parts, pivot_row)]
        for below in range(first + TILE, stop, TILE):
            tile = work[below : below + TILE, left:right]
            lower = columns(tile, first - left)
            pieces = [tile[:, span] for span in spans]
            for k, (inverse, pivot_row, heads) in enumerate(steps):
                multiplier = lower[k] * inverse
                for j in range(k + 1, TILE):
                    lower[j] = lower[j] - multiplier * heads[j]
                pieces = [piece - multiplier * row for piece, row in zip(pieces, pivot_row)]
            for span, piece in zip(spans, pieces):
                work[below : below + TILE, left + span.start : left + span.stop] = piece
        root = 1.0 / jnp.sqrt(diagonal)
        for span, part in zip(spans, parts):
            work[first : first + TILE, left + span.start : left + span.stop] = part * root


def take_out(work, start, stop, low, high, width):
    left = low // LANES * LANES
    right = width + (stop + LANES - 1) // LANES * LANES
    update = lax.dot_general(
        work[start:stop, left : (high + LANES - 1) // LANES * LANES],
        work[start:stop, left:right],
        (((0,), (0,)), ((), ())),
        precision=HIGHEST,
        preferred_element_type=F32,
    )
    work[low:high, left:right] = work[low:high, left:right] - update[low - left : high - left, :]


def factor_inverse(work, width):
    for start in range(0, width, PANEL):
        stop = start + PANEL
        factor_rows(work, start, stop, width)
        if stop < width:
            take_out(work, start, stop, stop, width, width)


def kernel(
    sizes, jac_hbm, probes_hbm, std_hbm, weight_hbm, sketch_out, inverse_out,
    jac, probes, std, weight, load_sems, std_col, weight_col, stacked, jt, jrecv, fsend, frecv, wbuf,
    gsend, gpair, gchunk, grecv, gfull, work, send_sems, recv_sems,
):
    n_obs, n_flux = sizes
    blocks, flux_local, probe_count = probes.shape
    obs_local = jac.shape[0]
    width = blocks * probe_count
    portion = flux_local // n_obs
    n_y = n_obs // 2
    chips = n_y * n_flux
    w_owners, w_rows = fsend.shape[0], fsend.shape[1]
    g_owners = gsend.shape[1]

    o, f = lax.axis_index("obs"), lax.axis_index("flux")
    core, y = lax.rem(o, 2), o // 2
    chip = y * n_flux + f
    partner = (o + 1 - 2 * core, f)
    w_mine = True if w_owners == n_flux else f < w_owners
    g_mine = True if g_owners == chips else chip < g_owners

    def on_chip(step, c):
        other = lax.rem(chip + step, chips)
        return other, ((other // n_flux) * 2 + c, lax.rem(other, n_flux))

    barrier = pltpu.get_barrier_semaphore()

    def greet(step):
        _, device = on_chip(step, core)
        pl.semaphore_signal(barrier, inc=1, device_id=device, device_id_type=MESH)

    def greet_other(step):
        _, device = on_chip(step, 1 - core)
        pl.semaphore_signal(barrier, inc=1, device_id=device, device_id_type=MESH)

    each(1, chips, greet)
    each(0, chips, greet_other)

    loads = [
        pltpu.make_async_copy(src, dst, load_sems.at[i])
        for i, (src, dst) in enumerate(
            ((std_hbm, std), (weight_hbm, weight), (probes_hbm, probes), (jac_hbm, jac))
        )
    ]
    for load in loads:
        load.start()
    loads[0].wait()
    loads[1].wait()
    for s in range(flux_local // LANES):
        part = slice(s * LANES, (s + 1) * LANES)
        std_col[part, :] = column(std[:, part])
    for s in range(obs_local // LANES):
        part = slice(s * LANES, (s + 1) * LANES)
        weight_col[part, :] = column(weight[:, part])
    loads[2].wait()
    for b in range(blocks):
        stacked[:, b * probe_count : (b + 1) * probe_count] = (
            probes[b].astype(F32) * std_col[...]
        ).astype(BF16)
    loads[3].wait()
    partial = jnp.dot(jac[...], stacked[...], preferred_element_type=F32)
    fsend[...] = partial.reshape(w_owners, w_rows, width)
    jt[...] = jac[...].T.reshape(n_obs, portion, obs_local)

    pl.semaphore_wait(barrier, 2 * chips - 1)

    def send(src, dst, number, device):
        copy = pltpu.make_async_remote_copy(
            src_ref=src, dst_ref=dst, send_sem=send_sems.at[number],
            recv_sem=recv_sems.at[number], device_id=device, device_id_type=MESH,
        )
        copy.start()
        return copy

    def send_forward(step):
        other = lax.rem(f + step, n_flux)
        only(
            True if w_owners == n_flux else other < w_owners,
            lambda: send(fsend.at[other], frecv.at[f], 0, (o, other)) and None,
        )

    each(1, n_flux, send_forward)

    def send_jacobian(step):
        other = lax.rem(o + step, n_obs)
        send(jt.at[other], jrecv.at[core, y], 1, (other, f))

    each(1, n_obs, send_jacobian)
    jrecv[core, y] = jt[o]

    def weigh():
        frecv[f] = fsend[f]
        wait_bytes(frecv.at[pl.ds(0, n_flux - 1)], recv_sems.at[0])
        rows = jnp.sum(frecv[...], axis=0)
        at = pl.ds(pl.multiple_of(f * w_rows, w_rows), w_rows)
        factor = jnp.concatenate([weight_col[at, :]] * (width // LANES), axis=1)
        mine = y * w_owners + f
        wbuf[core, mine] = (rows * factor).astype(BF16)

        def share(step):
            _, device = on_chip(step, core)
            send(wbuf.at[core, mine], wbuf.at[core, mine], 2, device)

        each(1, chips, share)

    only(w_mine, weigh)
    w_total = n_y * w_owners
    if w_mine is True:
        wait_bytes(wbuf.at[core, pl.ds(0, w_total - 1)], recv_sems.at[2])
    else:
        pl.when(w_mine)(lambda: wait_bytes(wbuf.at[core, pl.ds(0, w_total - 1)], recv_sems.at[2]))
        pl.when(f >= w_owners)(lambda: wait_bytes(wbuf.at[core], recv_sems.at[2]))
    across = send(wbuf.at[core], wbuf.at[core], 3, partner)

    wait_bytes(jt.at[pl.ds(0, n_obs - 1)], recv_sems.at[1])

    def adjoint(c):
        total = jnp.zeros((portion, width), F32)
        for row in range(n_y):
            piece = wbuf[c, row * w_owners : (row + 1) * w_owners].reshape(obs_local, width)
            total = total + jnp.dot(jrecv[c, row], piece, preferred_element_type=F32)
        return total

    own_half = adjoint(core)
    across.wait_recv()
    total = own_half + adjoint(1 - core)
    at = pl.ds(pl.multiple_of(o * portion, portion), portion)
    sketch = total * jnp.concatenate([std_col[at, :]] * (width // LANES), axis=1)
    sketch_out[...] = sketch
    gram = lax.dot_general(
        sketch, sketch, (((0,), (0,)), ((), ())), precision=HIGHEST, preferred_element_type=F32
    )
    gsend[...] = gram.reshape(gsend.shape)

    pair = send(gsend.at[1 - core], gpair, 4, partner)
    pair.wait_recv()
    gchunk[...] = gsend[core] + gpair[...]

    def send_gram(step):
        other, device = on_chip(step, core)
        only(
            True if g_owners == chips else other < g_owners,
            lambda: send(gchunk.at[other], grecv.at[chip], 5, device) and None,
        )

    each(1, chips, send_gram)

    def total_gram():
        grecv[chip] = gchunk[chip]
        wait_bytes(grecv.at[pl.ds(0, chips - 1)], recv_sems.at[5])
        gfull[core, chip] = jnp.sum(grecv[...], axis=0)

        def share(step):
            _, device = on_chip(step, core)
            send(gfull.at[core, chip], gfull.at[core, chip], 6, device)

        each(1, chips, share)

    only(g_mine, total_gram)
    if g_mine is True:
        wait_bytes(gfull.at[core, pl.ds(0, g_owners - 1)], recv_sems.at[6])
    else:
        pl.when(g_mine)(lambda: wait_bytes(gfull.at[core, pl.ds(0, g_owners - 1)], recv_sems.at[6]))
        pl.when(chip >= g_owners)(lambda: wait_bytes(gfull.at[core], recv_sems.at[6]))
    gacross = send(gfull.at[core], gfull.at[core], 7, partner)
    gacross.wait_recv()

    work[:, :width] = gfull[...].reshape(width, width)
    work[:, width:] = (
        lax.broadcasted_iota(jnp.int32, (width, width), 0)
        == lax.broadcasted_iota(jnp.int32, (width, width), 1)
    ).astype(F32)
    factor_inverse(work, width)
    inverse_out[...] = work[:, width:]

    if w_mine is True:
        wait_bytes(fsend.at[pl.ds(0, w_owners - 1)], send_sems.at[0])
        wait_bytes(grecv.at[pl.ds(0, 0 + chips - 1)], send_sems.at[5])
    else:
        pl.when(w_mine)(lambda: wait_bytes(fsend.at[pl.ds(0, w_owners - 1)], send_sems.at[0]))
        pl.when(f >= w_owners)(lambda: wait_bytes(fsend, send_sems.at[0]))
        pl.when(g_mine)(lambda: wait_bytes(gchunk.at[pl.ds(0, g_owners - 1)], send_sems.at[5]))
        pl.when(chip >= g_owners)(lambda: wait_bytes(gchunk, send_sems.at[5]))
    wait_bytes(jt.at[pl.ds(0, n_obs - 1)], send_sems.at[1])

    def w_sent():
        each(1, chips, lambda step: wait_bytes(wbuf.at[core, 0], send_sems.at[2]))

    only(w_mine, w_sent)
    across.wait_send()
    pair.wait_send()

    def g_sent():
        each(1, chips, lambda step: wait_bytes(gfull.at[core, 0], send_sems.at[6]))

    only(g_mine, g_sent)
    gacross.wait_send()


def finish(scale, sketch, inverse, sketch_out, basis_out):
    sketch_out[...] = sketch[...]
    basis = lax.dot_general(
        sketch[...], inverse[...], (((1,), (1,)), ((), ())),
        precision=HIGHEST, preferred_element_type=F32,
    )
    basis_out[...] = basis * scale


def body(jacobian, probes, prior_std, obs_weight):
    blocks, flux_local, probe_count = probes.shape
    obs_local = jacobian.shape[0]
    n_obs, n_flux = lax.axis_size("obs"), lax.axis_size("flux")
    width = blocks * probe_count
    portion = flux_local // n_obs
    chips = n_obs // 2 * n_flux
    w_rows = max(16, obs_local // n_flux)
    w_owners = obs_local // w_rows
    g_rows = max(8, width // 2 // chips)
    g_owners = width // 2 // g_rows
    scale = math.sqrt(flux_local * n_flux)
    vmem = pl.BlockSpec(memory_space=pltpu.VMEM)
    out = jax.ShapeDtypeStruct((portion, width), F32)
    sketch, inverse = pl.pallas_call(
        functools.partial(kernel, (n_obs, n_flux)),
        out_shape=(out, jax.ShapeDtypeStruct((width, width), F32)),
        in_specs=[pl.BlockSpec(memory_space=pl.ANY)] * 4,
        out_specs=(vmem, vmem),
        scratch_shapes=[
            pltpu.VMEM(jacobian.shape, BF16),
            pltpu.VMEM(probes.shape, BF16),
            pltpu.VMEM((1, flux_local), F32),
            pltpu.VMEM((1, obs_local), F32),
            pltpu.SemaphoreType.DMA((4,)),
            pltpu.VMEM((flux_local, LANES), F32),
            pltpu.VMEM((obs_local, LANES), F32),
            pltpu.VMEM((flux_local, width), BF16),
            pltpu.VMEM((n_obs, portion, obs_local), BF16),
            pltpu.VMEM((2, n_obs // 2, portion, obs_local), BF16),
            pltpu.VMEM((w_owners, w_rows, width), F32),
            pltpu.VMEM((n_flux, w_rows, width), F32),
            pltpu.VMEM((2, n_obs // 2 * w_owners, w_rows, width), BF16),
            pltpu.VMEM((2, g_owners, g_rows, width), F32),
            pltpu.VMEM((g_owners, g_rows, width), F32),
            pltpu.VMEM((g_owners, g_rows, width), F32),
            pltpu.VMEM((chips, g_rows, width), F32),
            pltpu.VMEM((2, g_owners, g_rows, width), F32),
            pltpu.VMEM((width, 2 * width), F32),
            pltpu.SemaphoreType.DMA((8,)),
            pltpu.SemaphoreType.DMA((8,)),
        ],
        compiler_params=pltpu.CompilerParams(collective_id=0, has_side_effects=True),
    )(jacobian, probes, prior_std.reshape(1, -1), obs_weight.reshape(1, -1))
    return pl.pallas_call(
        functools.partial(finish, scale),
        out_shape=(out, out),
        in_specs=[vmem] * 2,
        out_specs=(vmem, vmem),
    )(sketch, inverse)


def solution(mesh):
    in_specs = (P("obs", "flux"), P(None, "flux", None), P("flux"), P("obs"))
    out_specs = (P(("flux", "obs"), None), P(("flux", "obs"), None))
    return jax.shard_map(body, mesh=mesh, in_specs=in_specs, out_specs=out_specs, check_vma=False)
```

```python
import functools
import math

import jax
import jax.numpy as jnp
from jax import lax
from jax.experimental import pallas as pl
from jax.experimental.pallas import tpu as pltpu
from jax.sharding import PartitionSpec as P

MESH = pl.DeviceIdType.MESH
HIGHEST = lax.Precision.HIGHEST
F32 = jnp.float32
BF16 = jnp.bfloat16
LANES = 128
PANEL = 64
TILE = 8


def each(lower, upper, step):
    if upper - lower <= 16:
        for value in range(lower, upper):
            step(value)
    else:
        lax.fori_loop(lower, upper, lambda value, carry: (step(value), carry)[1], 0)


def only(condition, step):
    if condition is True:
        step()
    else:
        pl.when(condition)(step)


def wait_bytes(ref, sem):
    pltpu.make_async_copy(ref, ref, sem).wait()


def column(row):
    return jnp.broadcast_to(row, (LANES, LANES)).T


def factor_rows(work, start, stop, width):
    index = lax.broadcasted_iota(jnp.int32, (TILE, LANES), 0)

    def spread(x, k):
        return jnp.broadcast_to(x[k : k + 1, :], x.shape)

    def columns(x, at):
        return [jnp.broadcast_to(x[:, at + j : at + j + 1], (TILE, LANES)) for j in range(TILE)]

    for first in range(start, stop, TILE):
        left = first // LANES * LANES
        right = width + left + LANES
        spans = [slice(s, s + LANES) for s in range(0, right - left, LANES)]
        top = work[first : first + TILE, left:right]
        cols = columns(top, first - left)
        parts = [top[:, span] for span in spans]
        steps = []
        diagonal = jnp.ones((TILE, LANES), F32)
        for k in range(TILE):
            pivot = spread(cols[k], k)
            diagonal = jnp.where(index == k, pivot, diagonal)
            inverse = 1.0 / pivot
            pivot_row = [spread(part, k) for part in parts]
            heads = [spread(col, k) for col in cols]
            steps.append((inverse, pivot_row, heads))
            if k < TILE - 1:
                multiplier = jnp.where(index > k, cols[k], 0.0) * inverse
                for j in range(k + 1, TILE):
                    cols[j] = cols[j] - multiplier * heads[j]
                parts = [part - multiplier * row for part, row in zip(parts, pivot_row)]
        for below in range(first + TILE, stop, TILE):
            tile = work[below : below + TILE, left:right]
            lower = columns(tile, first - left)
            pieces = [tile[:, span] for span in spans]
            for k, (inverse, pivot_row, heads) in enumerate(steps):
                multiplier = lower[k] * inverse
                for j in range(k + 1, TILE):
                    lower[j] = lower[j] - multiplier * heads[j]
                pieces = [piece - multiplier * row for piece, row in zip(pieces, pivot_row)]
            for span, piece in zip(spans, pieces):
                work[below : below + TILE, left + span.start : left + span.stop] = piece
        root = 1.0 / jnp.sqrt(diagonal)
        for span, part in zip(spans, parts):
            work[first : first + TILE, left + span.start : left + span.stop] = part * root


def take_out(work, start, stop, low, high, width):
    left = low // LANES * LANES
    right = width + (stop + LANES - 1) // LANES * LANES
    update = lax.dot_general(
        work[start:stop, left : (high + LANES - 1) // LANES * LANES],
        work[start:stop, left:right],
        (((0,), (0,)), ((), ())),
        precision=HIGHEST,
        preferred_element_type=F32,
    )
    work[low:high, left:right] = work[low:high, left:right] - update[low - left : high - left, :]


def kernel(
    sizes, jac_hbm, probes_hbm, std_hbm, weight_hbm, sketch_out, inverse_out,
    jac, probes, std, weight, load_sems, std_col, weight_col, stacked, jt, jrecv, fsend, frecv, wbuf,
    gsend, gpair, gchunk, grecv, gfull,
    tsend, tpair, tchunk, trecv, tfull, work, send_sems, recv_sems,
):
    n_obs, n_flux = sizes
    blocks, flux_local, probe_count = probes.shape
    obs_local = jac.shape[0]
    width = blocks * probe_count
    portion = flux_local // n_obs
    n_y = n_obs // 2
    chips = n_y * n_flux
    w_owners, w_rows = fsend.shape[0], fsend.shape[1]
    g_owners = gsend.shape[1]

    o, f = lax.axis_index("obs"), lax.axis_index("flux")
    core, y = lax.rem(o, 2), o // 2
    chip = y * n_flux + f
    partner = (o + 1 - 2 * core, f)
    w_mine = True if w_owners == n_flux else f < w_owners
    g_mine = True if g_owners == chips else chip < g_owners

    def on_chip(step, c):
        other = lax.rem(chip + step, chips)
        return other, ((other // n_flux) * 2 + c, lax.rem(other, n_flux))

    barrier = pltpu.get_barrier_semaphore()

    def greet(step):
        _, device = on_chip(step, core)
        pl.semaphore_signal(barrier, inc=1, device_id=device, device_id_type=MESH)

    def greet_other(step):
        _, device = on_chip(step, 1 - core)
        pl.semaphore_signal(barrier, inc=1, device_id=device, device_id_type=MESH)

    each(1, chips, greet)
    each(0, chips, greet_other)

    loads = [
        pltpu.make_async_copy(src, dst, load_sems.at[i])
        for i, (src, dst) in enumerate(
            ((std_hbm, std), (weight_hbm, weight), (probes_hbm, probes), (jac_hbm, jac))
        )
    ]
    for load in loads:
        load.start()
    loads[0].wait()
    loads[1].wait()
    for s in range(flux_local // LANES):
        part = slice(s * LANES, (s + 1) * LANES)
        std_col[part, :] = column(std[:, part])
    for s in range(obs_local // LANES):
        part = slice(s * LANES, (s + 1) * LANES)
        weight_col[part, :] = column(weight[:, part])
    loads[2].wait()
    for b in range(blocks):
        stacked[:, b * probe_count : (b + 1) * probe_count] = (
            probes[b].astype(F32) * std_col[...]
        ).astype(BF16)
    loads[3].wait()
    partial = jnp.dot(jac[...], stacked[...], preferred_element_type=F32)
    fsend[...] = partial.reshape(w_owners, w_rows, width)
    jt[...] = jac[...].T.reshape(n_obs, portion, obs_local)

    pl.semaphore_wait(barrier, 2 * chips - 1)

    def send(src, dst, number, device):
        copy = pltpu.make_async_remote_copy(
            src_ref=src, dst_ref=dst, send_sem=send_sems.at[number],
            recv_sem=recv_sems.at[number], device_id=device, device_id_type=MESH,
        )
        copy.start()
        return copy

    def send_forward(step):
        other = lax.rem(f + step, n_flux)
        only(
            True if w_owners == n_flux else other < w_owners,
            lambda: send(fsend.at[other], frecv.at[f], 0, (o, other)) and None,
        )

    each(1, n_flux, send_forward)

    def send_jacobian(step):
        other = lax.rem(o + step, n_obs)
        send(jt.at[other], jrecv.at[core, y], 1, (other, f))

    each(1, n_obs, send_jacobian)
    jrecv[core, y] = jt[o]

    def weigh():
        frecv[f] = fsend[f]
        wait_bytes(frecv.at[pl.ds(0, n_flux - 1)], recv_sems.at[0])
        rows = jnp.sum(frecv[...], axis=0)
        at = pl.ds(pl.multiple_of(f * w_rows, w_rows), w_rows)
        factor = jnp.concatenate([weight_col[at, :]] * (width // LANES), axis=1)
        mine = y * w_owners + f
        wbuf[core, mine] = (rows * factor).astype(BF16)

        def share(step):
            _, device = on_chip(step, core)
            send(wbuf.at[core, mine], wbuf.at[core, mine], 2, device)

        each(1, chips, share)

    only(w_mine, weigh)
    w_total = n_y * w_owners
    if w_mine is True:
        wait_bytes(wbuf.at[core, pl.ds(0, w_total - 1)], recv_sems.at[2])
    else:
        pl.when(w_mine)(lambda: wait_bytes(wbuf.at[core, pl.ds(0, w_total - 1)], recv_sems.at[2]))
        pl.when(f >= w_owners)(lambda: wait_bytes(wbuf.at[core], recv_sems.at[2]))
    across = send(wbuf.at[core], wbuf.at[core], 3, partner)

    wait_bytes(jt.at[pl.ds(0, n_obs - 1)], recv_sems.at[1])

    def adjoint(c):
        total = jnp.zeros((portion, width), F32)
        for row in range(n_y):
            piece = wbuf[c, row * w_owners : (row + 1) * w_owners].reshape(obs_local, width)
            total = total + jnp.dot(jrecv[c, row], piece, preferred_element_type=F32)
        return total

    own_half = adjoint(core)
    across.wait_recv()
    total = own_half + adjoint(1 - core)
    at = pl.ds(pl.multiple_of(o * portion, portion), portion)
    sketch = total * jnp.concatenate([std_col[at, :]] * (width // LANES), axis=1)
    sketch_out[...] = sketch
    half = width // 2

    def gram(low, high):
        return lax.dot_general(
            sketch[:, low : low + half], sketch[:, high : high + half],
            (((0,), (0,)), ((), ())), precision=HIGHEST, preferred_element_type=F32,
        )

    gsend[0] = gram(0, 0).reshape(gsend.shape[1:])
    gsend[1] = gram(0, half).reshape(gsend.shape[1:])
    pair = send(gsend.at[1 - core], gpair, 4, partner)
    tsend[...] = gram(half, half).reshape(tsend.shape)
    tpair_copy = send(tsend.at[1 - core], tpair, 8, partner)

    pair.wait_recv()
    gchunk[...] = gsend[core] + gpair[...]

    def send_gram(step):
        other, device = on_chip(step, core)
        only(
            True if g_owners == chips else other < g_owners,
            lambda: send(gchunk.at[other], grecv.at[chip], 5, device) and None,
        )

    each(1, chips, send_gram)

    tpair_copy.wait_recv()
    tchunk[...] = tsend[core] + tpair[...]
    t_owners = tchunk.shape[0]
    piece = chip // 2
    t_mine = (chip == 2 * piece + lax.rem(piece, 2)) & (piece < t_owners)

    def send_tail(step):
        owned = lax.rem(piece + step, t_owners)
        owner = 2 * owned + lax.rem(owned, 2)
        device = ((owner // n_flux) * 2 + core, lax.rem(owner, n_flux))
        only(
            owner != chip,
            lambda: send(tchunk.at[owned], trecv.at[chip], 9, device) and None,
        )

    each(0, t_owners, send_tail)

    def total_gram():
        grecv[chip] = gchunk[chip]
        wait_bytes(grecv.at[pl.ds(0, chips - 1)], recv_sems.at[5])
        gfull[core, chip] = jnp.sum(grecv[...], axis=0)

        def share(step):
            _, device = on_chip(step, core)
            send(gfull.at[core, chip], gfull.at[core, chip], 6, device)

        each(1, chips, share)

    only(g_mine, total_gram)
    work[:, width:] = (
        lax.broadcasted_iota(jnp.int32, (width, width), 0)
        == lax.broadcasted_iota(jnp.int32, (width, width), 1)
    ).astype(F32)

    def total_tail():
        trecv[chip] = tchunk[piece]
        wait_bytes(trecv.at[pl.ds(0, chips - 1)], recv_sems.at[9])
        tfull[core * t_owners + piece] = jnp.sum(trecv[...], axis=0)

        def share(step, c):
            _, device = on_chip(step, c)
            send(tfull.at[core * t_owners + piece], tfull.at[core * t_owners + piece], 10, device)

        each(1, chips, lambda step: share(step, core))
        each(0, chips, lambda step: share(step, 1 - core))

    if g_mine is True:
        wait_bytes(gfull.at[core, pl.ds(0, g_owners - 1)], recv_sems.at[6])
    else:
        pl.when(g_mine)(lambda: wait_bytes(gfull.at[core, pl.ds(0, g_owners - 1)], recv_sems.at[6]))
        pl.when(chip >= g_owners)(lambda: wait_bytes(gfull.at[core], recv_sems.at[6]))
    gacross = send(gfull.at[core], gfull.at[core], 7, partner)
    only(t_mine, total_tail)
    gacross.wait_recv()

    work[:half, :half] = gfull[0].reshape(half, half)
    work[:half, half:width] = gfull[1].reshape(half, half)
    for start in range(0, half, PANEL):
        factor_rows(work, start, start + PANEL, width)
        if start + PANEL < half:
            take_out(work, start, start + PANEL, start + PANEL, half, width)

    pl.when(t_mine)(lambda: wait_bytes(tfull.at[pl.ds(0, 2 * t_owners - 1)], recv_sems.at[10]))
    pl.when(jnp.logical_not(t_mine))(lambda: wait_bytes(tfull, recv_sems.at[10]))
    work[half:, half:width] = tfull[...].reshape(half, half)
    take_out(work, 0, half, half, width, width)
    for start in range(half, width, PANEL):
        factor_rows(work, start, start + PANEL, width)
        if start + PANEL < width:
            take_out(work, start, start + PANEL, start + PANEL, width, width)
    inverse_out[...] = work[:, width:]

    if w_mine is True:
        wait_bytes(fsend.at[pl.ds(0, w_owners - 1)], send_sems.at[0])
        wait_bytes(grecv.at[pl.ds(0, 0 + chips - 1)], send_sems.at[5])
    else:
        pl.when(w_mine)(lambda: wait_bytes(fsend.at[pl.ds(0, w_owners - 1)], send_sems.at[0]))
        pl.when(f >= w_owners)(lambda: wait_bytes(fsend, send_sems.at[0]))
        pl.when(g_mine)(lambda: wait_bytes(gchunk.at[pl.ds(0, g_owners - 1)], send_sems.at[5]))
        pl.when(chip >= g_owners)(lambda: wait_bytes(gchunk, send_sems.at[5]))
    wait_bytes(jt.at[pl.ds(0, n_obs - 1)], send_sems.at[1])

    def w_sent():
        each(1, chips, lambda step: wait_bytes(wbuf.at[core, 0], send_sems.at[2]))

    only(w_mine, w_sent)
    across.wait_send()
    pair.wait_send()

    def g_sent():
        each(1, chips, lambda step: wait_bytes(gfull.at[core, 0], send_sems.at[6]))

    only(g_mine, g_sent)
    gacross.wait_send()
    tpair_copy.wait_send()

    def tail_sent(count):
        each(0, count, lambda step: wait_bytes(tchunk.at[0], send_sems.at[9]))

    pl.when(t_mine)(lambda: tail_sent(t_owners - 1))
    pl.when(jnp.logical_not(t_mine))(lambda: tail_sent(t_owners))
    pl.when(t_mine)(
        lambda: each(1, 2 * chips, lambda step: wait_bytes(tchunk.at[0], send_sems.at[10]))
    )


def finish(scale, sketch, inverse, sketch_out, basis_out):
    sketch_out[...] = sketch[...]
    basis = lax.dot_general(
        sketch[...], inverse[...], (((1,), (1,)), ((), ())),
        precision=HIGHEST, preferred_element_type=F32,
    )
    basis_out[...] = basis * scale


def body(jacobian, probes, prior_std, obs_weight):
    blocks, flux_local, probe_count = probes.shape
    obs_local = jacobian.shape[0]
    n_obs, n_flux = lax.axis_size("obs"), lax.axis_size("flux")
    width = blocks * probe_count
    portion = flux_local // n_obs
    chips = n_obs // 2 * n_flux
    w_rows = max(16, obs_local // n_flux)
    w_owners = obs_local // w_rows
    half = width // 2
    g_rows = max(TILE, half // chips)
    g_owners = half // g_rows
    t_owners = half // 2 // TILE
    scale = math.sqrt(flux_local * n_flux)
    vmem = pl.BlockSpec(memory_space=pltpu.VMEM)
    out = jax.ShapeDtypeStruct((portion, width), F32)
    sketch, inverse = pl.pallas_call(
        functools.partial(kernel, (n_obs, n_flux)),
        out_shape=(out, jax.ShapeDtypeStruct((width, width), F32)),
        in_specs=[pl.BlockSpec(memory_space=pl.ANY)] * 4,
        out_specs=(vmem, vmem),
        scratch_shapes=[
            pltpu.VMEM(jacobian.shape, BF16),
            pltpu.VMEM(probes.shape, BF16),
            pltpu.VMEM((1, flux_local), F32),
            pltpu.VMEM((1, obs_local), F32),
            pltpu.SemaphoreType.DMA((4,)),
            pltpu.VMEM((flux_local, LANES), F32),
            pltpu.VMEM((obs_local, LANES), F32),
            pltpu.VMEM((flux_local, width), BF16),
            pltpu.VMEM((n_obs, portion, obs_local), BF16),
            pltpu.VMEM((2, n_obs // 2, portion, obs_local), BF16),
            pltpu.VMEM((w_owners, w_rows, width), F32),
            pltpu.VMEM((n_flux, w_rows, width), F32),
            pltpu.VMEM((2, n_obs // 2 * w_owners, w_rows, width), BF16),
            pltpu.VMEM((2, g_owners, g_rows, half), F32),
            pltpu.VMEM((g_owners, g_rows, half), F32),
            pltpu.VMEM((g_owners, g_rows, half), F32),
            pltpu.VMEM((chips, g_rows, half), F32),
            pltpu.VMEM((2, g_owners, g_rows, half), F32),
            pltpu.VMEM((2, t_owners, TILE, half), F32),
            pltpu.VMEM((t_owners, TILE, half), F32),
            pltpu.VMEM((t_owners, TILE, half), F32),
            pltpu.VMEM((chips, TILE, half), F32),
            pltpu.VMEM((2 * t_owners, TILE, half), F32),
            pltpu.VMEM((width, 2 * width), F32),
            pltpu.SemaphoreType.DMA((11,)),
            pltpu.SemaphoreType.DMA((11,)),
        ],
        compiler_params=pltpu.CompilerParams(collective_id=0, has_side_effects=True),
    )(jacobian, probes, prior_std.reshape(1, -1), obs_weight.reshape(1, -1))
    return pl.pallas_call(
        functools.partial(finish, scale),
        out_shape=(out, out),
        in_specs=[vmem] * 2,
        out_specs=(vmem, vmem),
    )(sketch, inverse)


def solution(mesh):
    in_specs = (P("obs", "flux"), P(None, "flux", None), P("flux"), P("obs"))
    out_specs = (P(("flux", "obs"), None), P(("flux", "obs"), None))
    return jax.shard_map(body, mesh=mesh, in_specs=in_specs, out_specs=out_specs, check_vma=False)
```

```python
import functools
import math

import jax
import jax.numpy as jnp
from jax import lax
from jax.experimental import pallas as pl
from jax.experimental.pallas import tpu as pltpu
from jax.sharding import PartitionSpec as P

MESH = pl.DeviceIdType.MESH
HIGHEST = lax.Precision.HIGHEST
F32 = jnp.float32
BF16 = jnp.bfloat16
LANES = 128
PANEL = 64
TILE = 8
VMEM_LIMIT = 24 * 2**20


def each(lower, upper, step):
    if upper - lower <= 16:
        for value in range(lower, upper):
            step(value)
    else:
        lax.fori_loop(lower, upper, lambda value, carry: (step(value), carry)[1], 0)


def only(condition, step):
    if condition is True:
        step()
    else:
        pl.when(condition)(step)


def wait_bytes(ref, sem):
    pltpu.make_async_copy(ref, ref, sem).wait()


def column(row):
    return jnp.broadcast_to(row, (LANES, LANES)).T


def factor_rows(work, start, stop, width):
    index = lax.broadcasted_iota(jnp.int32, (TILE, LANES), 0)

    def spread(x, k):
        return jnp.broadcast_to(x[k : k + 1, :], x.shape)

    def columns(x, at):
        return [jnp.broadcast_to(x[:, at + j : at + j + 1], (TILE, LANES)) for j in range(TILE)]

    for first in range(start, stop, TILE):
        left = first // LANES * LANES
        right = width + left + LANES
        spans = [slice(s, s + LANES) for s in range(0, right - left, LANES)]
        top = work[first : first + TILE, left:right]
        cols = columns(top, first - left)
        parts = [top[:, span] for span in spans]
        steps = []
        diagonal = jnp.ones((TILE, LANES), F32)
        for k in range(TILE):
            pivot = spread(cols[k], k)
            diagonal = jnp.where(index == k, pivot, diagonal)
            inverse = 1.0 / pivot
            pivot_row = [spread(part, k) for part in parts]
            heads = [spread(col, k) for col in cols]
            steps.append((inverse, pivot_row, heads))
            if k < TILE - 1:
                multiplier = jnp.where(index > k, cols[k], 0.0) * inverse
                for j in range(k + 1, TILE):
                    cols[j] = cols[j] - multiplier * heads[j]
                parts = [part - multiplier * row for part, row in zip(parts, pivot_row)]
        for below in range(first + TILE, stop, TILE):
            tile = work[below : below + TILE, left:right]
            lower = columns(tile, first - left)
            pieces = [tile[:, span] for span in spans]
            for k, (inverse, pivot_row, heads) in enumerate(steps):
                multiplier = lower[k] * inverse
                for j in range(k + 1, TILE):
                    lower[j] = lower[j] - multiplier * heads[j]
                pieces = [piece - multiplier * row for piece, row in zip(pieces, pivot_row)]
            for span, piece in zip(spans, pieces):
                work[below : below + TILE, left + span.start : left + span.stop] = piece
        root = 1.0 / jnp.sqrt(diagonal)
        for span, part in zip(spans, parts):
            work[first : first + TILE, left + span.start : left + span.stop] = part * root


def take_out(work, start, stop, low, high, width):
    left = low // LANES * LANES
    right = width + (stop + LANES - 1) // LANES * LANES
    update = lax.dot_general(
        work[start:stop, left : (high + LANES - 1) // LANES * LANES],
        work[start:stop, left:right],
        (((0,), (0,)), ((), ())),
        precision=HIGHEST,
        preferred_element_type=F32,
    )
    work[low:high, left:right] = work[low:high, left:right] - update[low - left : high - left, :]


def kernel(
    sizes, jac_hbm, probes_hbm, std_hbm, weight_hbm, sketch_out, inverse_out,
    jac, probes, std, weight, load_sems, std_col, weight_col, stacked, jt, jrecv, fsend, frecv, wbuf,
    gsend, gpair, gchunk, grecv, gfull,
    tsend, tpair, tchunk, trecv, tfull, work, send_sems, recv_sems,
):
    n_obs, n_flux = sizes
    blocks, flux_local, probe_count = probes.shape
    obs_local = jac.shape[0]
    width = blocks * probe_count
    portion = flux_local // n_obs
    n_y = n_obs // 2
    chips = n_y * n_flux
    w_owners, w_rows = fsend.shape[0], fsend.shape[1]
    g_owners = gsend.shape[1]

    o, f = lax.axis_index("obs"), lax.axis_index("flux")
    core, y = lax.rem(o, 2), o // 2
    chip = y * n_flux + f
    partner = (o + 1 - 2 * core, f)
    w_mine = True if w_owners == n_flux else f < w_owners
    g_mine = True if g_owners == chips else chip < g_owners

    def on_chip(step, c):
        other = lax.rem(chip + step, chips)
        return other, ((other // n_flux) * 2 + c, lax.rem(other, n_flux))

    barrier = pltpu.get_barrier_semaphore()

    def greet(step):
        _, device = on_chip(step, core)
        pl.semaphore_signal(barrier, inc=1, device_id=device, device_id_type=MESH)

    def greet_other(step):
        _, device = on_chip(step, 1 - core)
        pl.semaphore_signal(barrier, inc=1, device_id=device, device_id_type=MESH)

    each(1, chips, greet)
    each(0, chips, greet_other)

    loads = [
        pltpu.make_async_copy(src, dst, load_sems.at[i])
        for i, (src, dst) in enumerate(
            ((std_hbm, std), (weight_hbm, weight), (probes_hbm, probes), (jac_hbm, jac))
        )
    ]
    for load in loads:
        load.start()
    loads[0].wait()
    loads[1].wait()
    for s in range(flux_local // LANES):
        part = slice(s * LANES, (s + 1) * LANES)
        std_col[part, :] = column(std[:, part])
    for s in range(obs_local // LANES):
        part = slice(s * LANES, (s + 1) * LANES)
        weight_col[part, :] = column(weight[:, part])
    loads[2].wait()
    for b in range(blocks):
        stacked[:, b * probe_count : (b + 1) * probe_count] = (
            probes[b].astype(F32) * std_col[...]
        ).astype(BF16)
    loads[3].wait()
    partial = jnp.dot(jac[...], stacked[...], preferred_element_type=F32)
    fsend[...] = partial.reshape(w_owners, w_rows, width)
    jt[...] = jac[...].T.reshape(n_obs, portion, obs_local)

    pl.semaphore_wait(barrier, 2 * chips - 1)

    def send(src, dst, number, device):
        copy = pltpu.make_async_remote_copy(
            src_ref=src, dst_ref=dst, send_sem=send_sems.at[number],
            recv_sem=recv_sems.at[number], device_id=device, device_id_type=MESH,
        )
        copy.start()
        return copy

    def send_forward(step):
        other = lax.rem(f + step, n_flux)
        only(
            True if w_owners == n_flux else other < w_owners,
            lambda: send(fsend.at[other], frecv.at[f], 0, (o, other)) and None,
        )

    each(1, n_flux, send_forward)

    def send_jacobian(step):
        other = lax.rem(o + step, n_obs)
        send(jt.at[other], jrecv.at[core, y], 1, (other, f))

    each(1, n_obs, send_jacobian)
    jrecv[core, y] = jt[o]

    def weigh():
        frecv[f] = fsend[f]
        wait_bytes(frecv.at[pl.ds(0, n_flux - 1)], recv_sems.at[0])
        rows = jnp.sum(frecv[...], axis=0)
        at = pl.ds(pl.multiple_of(f * w_rows, w_rows), w_rows)
        factor = jnp.concatenate([weight_col[at, :]] * (width // LANES), axis=1)
        mine = y * w_owners + f
        wbuf[core, mine] = (rows * factor).astype(BF16)

        def share(step):
            _, device = on_chip(step, core)
            send(wbuf.at[core, mine], wbuf.at[core, mine], 2, device)

        each(1, chips, share)

    only(w_mine, weigh)
    w_total = n_y * w_owners
    if w_mine is True:
        wait_bytes(wbuf.at[core, pl.ds(0, w_total - 1)], recv_sems.at[2])
    else:
        pl.when(w_mine)(lambda: wait_bytes(wbuf.at[core, pl.ds(0, w_total - 1)], recv_sems.at[2]))
        pl.when(f >= w_owners)(lambda: wait_bytes(wbuf.at[core], recv_sems.at[2]))
    across = send(wbuf.at[core], wbuf.at[core], 3, partner)

    wait_bytes(jt.at[pl.ds(0, n_obs - 1)], recv_sems.at[1])

    def adjoint(c):
        total = jnp.zeros((portion, width), F32)
        for row in range(n_y):
            piece = wbuf[c, row * w_owners : (row + 1) * w_owners].reshape(obs_local, width)
            total = total + jnp.dot(jrecv[c, row], piece, preferred_element_type=F32)
        return total

    own_half = adjoint(core)
    across.wait_recv()
    total = own_half + adjoint(1 - core)
    at = pl.ds(pl.multiple_of(o * portion, portion), portion)
    sketch = total * jnp.concatenate([std_col[at, :]] * (width // LANES), axis=1)
    sketch_out[...] = sketch
    half = width // 2

    def gram(low, high):
        return lax.dot_general(
            sketch[:, low : low + half], sketch[:, high : high + half],
            (((0,), (0,)), ((), ())), precision=HIGHEST, preferred_element_type=F32,
        )

    gsend[0] = gram(0, 0).reshape(gsend.shape[1:])
    gsend[1] = gram(0, half).reshape(gsend.shape[1:])
    pair = send(gsend.at[1 - core], gpair, 4, partner)
    tsend[...] = gram(half, half).reshape(tsend.shape)
    tpair_copy = send(tsend.at[1 - core], tpair, 8, partner)

    pair.wait_recv()
    gchunk[...] = gsend[core] + gpair[...]

    def send_gram(step):
        other, device = on_chip(step, core)
        only(
            True if g_owners == chips else other < g_owners,
            lambda: send(gchunk.at[other], grecv.at[chip], 5, device) and None,
        )

    each(1, chips, send_gram)

    tpair_copy.wait_recv()
    tchunk[...] = tsend[core] + tpair[...]
    t_owners = tchunk.shape[0]
    piece = chip // 2
    t_mine = (chip == 2 * piece + lax.rem(piece, 2)) & (piece < t_owners)

    def send_tail(step):
        owned = lax.rem(piece + step, t_owners)
        owner = 2 * owned + lax.rem(owned, 2)
        device = ((owner // n_flux) * 2 + core, lax.rem(owner, n_flux))
        only(
            owner != chip,
            lambda: send(tchunk.at[owned], trecv.at[chip], 9, device) and None,
        )

    each(0, t_owners, send_tail)

    def total_gram():
        grecv[chip] = gchunk[chip]
        wait_bytes(grecv.at[pl.ds(0, chips - 1)], recv_sems.at[5])
        gfull[core, chip] = jnp.sum(grecv[...], axis=0)

        def share(step):
            _, device = on_chip(step, core)
            send(gfull.at[core, chip], gfull.at[core, chip], 6, device)

        each(1, chips, share)

    only(g_mine, total_gram)
    work[:, width:] = (
        lax.broadcasted_iota(jnp.int32, (width, width), 0)
        == lax.broadcasted_iota(jnp.int32, (width, width), 1)
    ).astype(F32)

    def total_tail():
        trecv[chip] = tchunk[piece]
        wait_bytes(trecv.at[pl.ds(0, chips - 1)], recv_sems.at[9])
        tfull[core * t_owners + piece] = jnp.sum(trecv[...], axis=0)

        def share(step, c):
            _, device = on_chip(step, c)
            send(tfull.at[core * t_owners + piece], tfull.at[core * t_owners + piece], 10, device)

        each(1, chips, lambda step: share(step, core))
        each(0, chips, lambda step: share(step, 1 - core))

    if g_mine is True:
        wait_bytes(gfull.at[core, pl.ds(0, g_owners - 1)], recv_sems.at[6])
    else:
        pl.when(g_mine)(lambda: wait_bytes(gfull.at[core, pl.ds(0, g_owners - 1)], recv_sems.at[6]))
        pl.when(chip >= g_owners)(lambda: wait_bytes(gfull.at[core], recv_sems.at[6]))
    gacross = send(gfull.at[core], gfull.at[core], 7, partner)
    only(t_mine, total_tail)
    gacross.wait_recv()

    work[:half, :half] = gfull[0].reshape(half, half)
    work[:half, half:width] = gfull[1].reshape(half, half)
    for start in range(0, half, PANEL):
        factor_rows(work, start, start + PANEL, width)
        if start + PANEL < half:
            take_out(work, start, start + PANEL, start + PANEL, half, width)

    pl.when(t_mine)(lambda: wait_bytes(tfull.at[pl.ds(0, 2 * t_owners - 1)], recv_sems.at[10]))
    pl.when(jnp.logical_not(t_mine))(lambda: wait_bytes(tfull, recv_sems.at[10]))
    work[half:, half:width] = tfull[...].reshape(half, half)
    take_out(work, 0, half, half, width, width)
    for start in range(half, width, PANEL):
        factor_rows(work, start, start + PANEL, width)
        if start + PANEL < width:
            take_out(work, start, start + PANEL, start + PANEL, width, width)
    inverse_out[...] = work[:, width:]

    if w_mine is True:
        wait_bytes(fsend.at[pl.ds(0, w_owners - 1)], send_sems.at[0])
        wait_bytes(grecv.at[pl.ds(0, 0 + chips - 1)], send_sems.at[5])
    else:
        pl.when(w_mine)(lambda: wait_bytes(fsend.at[pl.ds(0, w_owners - 1)], send_sems.at[0]))
        pl.when(f >= w_owners)(lambda: wait_bytes(fsend, send_sems.at[0]))
        pl.when(g_mine)(lambda: wait_bytes(gchunk.at[pl.ds(0, g_owners - 1)], send_sems.at[5]))
        pl.when(chip >= g_owners)(lambda: wait_bytes(gchunk, send_sems.at[5]))
    wait_bytes(jt.at[pl.ds(0, n_obs - 1)], send_sems.at[1])

    def w_sent():
        each(1, chips, lambda step: wait_bytes(wbuf.at[core, 0], send_sems.at[2]))

    only(w_mine, w_sent)
    across.wait_send()
    pair.wait_send()

    def g_sent():
        each(1, chips, lambda step: wait_bytes(gfull.at[core, 0], send_sems.at[6]))

    only(g_mine, g_sent)
    gacross.wait_send()
    tpair_copy.wait_send()

    def tail_sent(count):
        each(0, count, lambda step: wait_bytes(tchunk.at[0], send_sems.at[9]))

    pl.when(t_mine)(lambda: tail_sent(t_owners - 1))
    pl.when(jnp.logical_not(t_mine))(lambda: tail_sent(t_owners))
    pl.when(t_mine)(
        lambda: each(1, 2 * chips, lambda step: wait_bytes(tchunk.at[0], send_sems.at[10]))
    )


def finish(scale, sketch, inverse, sketch_out, basis_out):
    sketch_out[...] = sketch[...]
    basis = lax.dot_general(
        sketch[...], inverse[...], (((1,), (1,)), ((), ())),
        precision=HIGHEST, preferred_element_type=F32,
    )
    basis_out[...] = basis * scale


def body(jacobian, probes, prior_std, obs_weight):
    blocks, flux_local, probe_count = probes.shape
    obs_local = jacobian.shape[0]
    n_obs, n_flux = lax.axis_size("obs"), lax.axis_size("flux")
    width = blocks * probe_count
    portion = flux_local // n_obs
    chips = n_obs // 2 * n_flux
    w_rows = max(16, obs_local // n_flux)
    w_owners = obs_local // w_rows
    half = width // 2
    g_rows = max(TILE, half // chips)
    g_owners = half // g_rows
    t_owners = half // 2 // TILE
    scale = math.sqrt(flux_local * n_flux)
    vmem = pl.BlockSpec(memory_space=pltpu.VMEM)
    out = jax.ShapeDtypeStruct((portion, width), F32)
    sketch, inverse = pl.pallas_call(
        functools.partial(kernel, (n_obs, n_flux)),
        out_shape=(out, jax.ShapeDtypeStruct((width, width), F32)),
        in_specs=[pl.BlockSpec(memory_space=pltpu.HBM)] * 4,
        out_specs=(vmem, vmem),
        scratch_shapes=[
            pltpu.VMEM(jacobian.shape, BF16),
            pltpu.VMEM(probes.shape, BF16),
            pltpu.VMEM((1, flux_local), F32),
            pltpu.VMEM((1, obs_local), F32),
            pltpu.SemaphoreType.DMA((4,)),
            pltpu.VMEM((flux_local, LANES), F32),
            pltpu.VMEM((obs_local, LANES), F32),
            pltpu.VMEM((flux_local, width), BF16),
            pltpu.VMEM((n_obs, portion, obs_local), BF16),
            pltpu.VMEM((2, n_obs // 2, portion, obs_local), BF16),
            pltpu.VMEM((w_owners, w_rows, width), F32),
            pltpu.VMEM((n_flux, w_rows, width), F32),
            pltpu.VMEM((2, n_obs // 2 * w_owners, w_rows, width), BF16),
            pltpu.VMEM((2, g_owners, g_rows, half), F32),
            pltpu.VMEM((g_owners, g_rows, half), F32),
            pltpu.VMEM((g_owners, g_rows, half), F32),
            pltpu.VMEM((chips, g_rows, half), F32),
            pltpu.VMEM((2, g_owners, g_rows, half), F32),
            pltpu.VMEM((2, t_owners, TILE, half), F32),
            pltpu.VMEM((t_owners, TILE, half), F32),
            pltpu.VMEM((t_owners, TILE, half), F32),
            pltpu.VMEM((chips, TILE, half), F32),
            pltpu.VMEM((2 * t_owners, TILE, half), F32),
            pltpu.VMEM((width, 2 * width), F32),
            pltpu.SemaphoreType.DMA((11,)),
            pltpu.SemaphoreType.DMA((11,)),
        ],
        compiler_params=pltpu.CompilerParams(
            collective_id=0, has_side_effects=True, vmem_limit_bytes=VMEM_LIMIT
        ),
    )(jacobian, probes, prior_std.reshape(1, -1), obs_weight.reshape(1, -1))
    return pl.pallas_call(
        functools.partial(finish, scale),
        out_shape=(out, out),
        in_specs=[vmem] * 2,
        out_specs=(vmem, vmem),
        compiler_params=pltpu.CompilerParams(vmem_limit_bytes=VMEM_LIMIT),
    )(sketch, inverse)


def solution(mesh):
    in_specs = (P("obs", "flux"), P(None, "flux", None), P("flux"), P("obs"))
    out_specs = (P(("flux", "obs"), None), P(("flux", "obs"), None))
    return jax.shard_map(body, mesh=mesh, in_specs=in_specs, out_specs=out_specs, check_vma=False)
```
